32 devices in a mesh: row: 8 (over z, x), col: 4 (over y, core).
Axes of the slice: x: 2, y: 2, z: 4, core: 2. Of those that a mesh axis runs over, the one named last changes fastest.
Arguments:
- positions: float32 [3, 8192], P(None, ('row', 'col')), may hold values from -6 to 6
- features: bfloat16 [128, 8192], P(None, ('row', 'col')), may hold values from -6 to 6
- fill: int32 [64], P(('row', 'col')), may hold values from 64 to 128, as said below
- tiles: int32 [256, 2], P(('row', 'col')), may hold values from 0 to 15, as said below
- tile_count: int32 [32], P(('row', 'col')), may hold values from 2 to 8, as said below
- w_radial: float32 [64, 32], replicated, may hold values from -1 to 1
- w_left: bfloat16 [128, 64], replicated, may hold values from -0.5 to 0.5
- w_right: bfloat16 [128, 64], replicated, may hold values from -0.5 to 0.5
- w_hidden: bfloat16 [64, 64], replicated, may hold values from -0.75 to 0.75
- w_out: bfloat16 [64], replicated, may hold values from -0.25 to 0.25
Outputs:
- forces: float32 [3, 8192], P(None, ('row', 'col'))
- bead_energy: float32 [8192], P(('row', 'col'))
The draws below stay inside these ranges and needn't reach their ends.
Inputs may be any that keep to these rules, and one draw needn't show every extreme that they name: `fill`: at least 64; some cluster holds 128. `tiles`: A device's 8 slots name distinct cluster pairs; the first entry is below 8, the second below 16; some device has the pair of the last clusters of both groups. `tile_count`: at least 2; some device has all 8 slots live.
All inputs are finite; a program needn't handle non-finite values.
Results may differ from the reference program's by a relative error of at most 0.0045.
Values may be sent and summed in bfloat16 or wider, within the bound.
A program may use at most 64 MiB of HBM per device.

```python
import jax
import jax.numpy as jnp
from jax import lax

CL = 128
HID = 64
EMB = 128
NRBF = 32
CPD = 2
MAXT = 8
NC = 64
NB = 8192
GR = 8
GC = 16
NTILES = 256
N_COL = 4


def draw_fill(key, part):
    counts = jax.random.randint(jax.random.fold_in(key, 11), (NC,), CL // 2, CL + 1)
    where = jax.random.randint(jax.random.fold_in(key, 12), (), 0, NC)
    return counts.at[where].set(CL).astype(jnp.int32)


def draw_tiles(key, part):
    devices = NTILES // MAXT
    chosen = jax.random.randint(jax.random.fold_in(key, 22), (), 0, devices)
    corner = GR * GC - 1

    def one(index):
        order = jax.random.permutation(jax.random.fold_in(jax.random.fold_in(key, 21), index), GR * GC)[:MAXT]
        present = jnp.any(order == corner)
        forced = jnp.where(present, order, order.at[0].set(corner))
        order = jnp.where(index == chosen, forced, order)
        return jnp.stack([order // GC, order % GC], 1)
    return jax.vmap(one)(jnp.arange(devices)).reshape(NTILES, 2).astype(jnp.int32)


def draw_tile_count(key, part):
    devices = NTILES // MAXT
    counts = jax.random.randint(jax.random.fold_in(key, 31), (devices,), 2, MAXT + 1)
    where = jax.random.randint(jax.random.fold_in(key, 32), (), 0, devices)
    return counts.at[where].set(MAXT).astype(jnp.int32)


def steps_of(own_key, dims, shards, least, largest):
    level = 1.0
    for position, parts in shards:
        heights = jax.random.uniform(jax.random.fold_in(jax.random.fold_in(own_key, 6), position), (parts,), jnp.float32, least / len(shards), largest / len(shards))
        level = level * jnp.repeat(jnp.exp(heights), dims[position] // parts).reshape((-1,) + (1,) * (len(dims) - 1 - position))
    return level


def gaussian(rng, extent, deviation, limit, cuts=(), kind=jnp.bfloat16):
    level = steps_of(rng, extent, cuts, -0.22, 0.18) if cuts else 1.0
    drawn = jax.random.normal(rng, extent, jnp.float32) * deviation * level
    return jnp.minimum(jnp.maximum(drawn, -limit), limit).astype(kind)


def setup_inputs(seed: int = 0) -> dict:
    streams_of = jax.random.split(jax.random.key(seed), 11)
    positions = gaussian(streams_of[0], (3, NB), 1.0, 6.0, ((1, 32),), jnp.float32)
    features = gaussian(streams_of[1], (EMB, NB), 1.0, 6.0, ((1, 32),))
    fill = draw_fill(jax.random.fold_in(streams_of[10], 71), 0)
    tiles = draw_tiles(jax.random.fold_in(streams_of[10], 71), 0)
    tile_count = draw_tile_count(jax.random.fold_in(streams_of[10], 71), 0)
    w_radial = gaussian(streams_of[5], (HID, NRBF), NRBF ** -0.5, 1.0, (), jnp.float32)
    w_left = gaussian(streams_of[6], (EMB, HID), EMB ** -0.5, 0.5)
    w_right = gaussian(streams_of[7], (EMB, HID), EMB ** -0.5, 0.5)
    w_hidden = gaussian(streams_of[8], (HID, HID), HID ** -0.5, 0.75)
    w_out = gaussian(streams_of[9], (HID,), (HID * 8) ** -0.5, 0.25)
    return dict(positions=positions, features=features, fill=fill, tiles=tiles, tile_count=tile_count, w_radial=w_radial, w_left=w_left, w_right=w_right, w_hidden=w_hidden, w_out=w_out)


SOFT = 0.01
RANGE = 6.0

def dsilu(value):
    sig = jax.nn.sigmoid(value)
    return sig * (1.0 + value * (1.0 - sig))

def tile_terms(left, right, proj_a, proj_b, same, live_tile, w_radial, w_hidden, w_out):
    slots = left.shape[1]
    hidden = w_radial.shape[0]
    nbasis = w_radial.shape[1]
    delta = left[:3, :, None] - right[:3, None, :]
    dist = jnp.sqrt(lax.optimization_barrier(jnp.sum(delta * delta, 0)) + SOFT)
    ident = (jnp.arange(slots)[:, None] == jnp.arange(slots)[None, :]).astype(jnp.float32)
    mask = left[3][:, None] * right[3][None, :] * (1.0 - same * ident) * live_tile
    flat = dist.reshape(-1)
    centers = RANGE * jnp.arange(nbasis, dtype=jnp.float32) / (nbasis - 1)
    sharp = ((nbasis - 1) / RANGE) ** 2
    offset = flat[None, :] - centers[:, None]
    basis = jnp.exp(-sharp * offset * offset)
    pair_in = (proj_a.astype(jnp.float32)[:, :, None] + proj_b.astype(jnp.float32)[:, None, :]).reshape(hidden, -1)
    pre1 = jnp.dot(w_radial, basis, precision=lax.Precision.HIGHEST) + pair_in
    act1 = jax.nn.silu(pre1).astype(jnp.bfloat16)
    pre2 = jnp.dot(w_hidden, act1, preferred_element_type=jnp.float32)
    act2 = jax.nn.silu(pre2).astype(jnp.bfloat16)
    energy = jnp.dot(w_out[None, :], act2, preferred_element_type=jnp.float32)[0]
    back2 = (w_out.astype(jnp.float32)[:, None] * dsilu(pre2)).astype(jnp.bfloat16)
    back1 = lax.dot_general(w_hidden, back2, (((0,), (0,)), ((), ())), preferred_element_type=jnp.float32) * dsilu(pre1)
    radial = lax.dot_general(w_radial, back1, (((0,), (0,)), ((), ())), precision=lax.Precision.HIGHEST)
    slope = lax.optimization_barrier(jnp.sum(radial * basis * (-2.0 * sharp * offset), 0))
    weight = mask * slope.reshape(slots, slots) / dist
    energy_left = lax.optimization_barrier(jnp.sum(mask * energy.reshape(slots, slots), 1))
    pos_left = left[:3]
    pos_right = right[:3]
    force_left = jnp.dot(pos_right, weight.T, precision=lax.Precision.HIGHEST) - pos_left * lax.optimization_barrier(jnp.sum(weight, 1))[None, :]
    force_right = jnp.dot(pos_left, weight, precision=lax.Precision.HIGHEST) - pos_right * lax.optimization_barrier(jnp.sum(weight, 0))[None, :]
    return (force_left, energy_left, force_right)

def reference(positions, features, fill, tiles, tile_count, w_radial, w_left, w_right, w_hidden, w_out):
    live = (jnp.arange(CL, dtype=jnp.int32)[None, :] < fill[:, None]).astype(jnp.float32).reshape(NB)
    coords = jnp.concatenate([positions, live[None, :]], 0)
    proj_left = lax.dot_general(w_left, features, (((0,), (0,)), ((), ())), preferred_element_type=jnp.float32).astype(jnp.bfloat16)
    proj_right = lax.dot_general(w_right, features, (((0,), (0,)), ((), ())), preferred_element_type=jnp.float32).astype(jnp.bfloat16)

    def step(carry, slot):
        firsts, seconds = carry
        device = slot // MAXT
        row_index = device // N_COL
        col_index = device % N_COL
        first = (row_index * GR + tiles[slot, 0]).astype(jnp.int32)
        other = tiles[slot, 1]
        second = ((other // CPD * N_COL + col_index) * CPD + other % CPD).astype(jnp.int32)
        is_live = slot % MAXT < tile_count[device]

        def work(carry):
            firsts, seconds = carry
            start_a = (first * CL).astype(jnp.int32)
            start_b = (second * CL).astype(jnp.int32)
            left = lax.dynamic_slice_in_dim(coords, start_a, CL, 1)
            right = lax.dynamic_slice_in_dim(coords, start_b, CL, 1)
            part_a = lax.dynamic_slice_in_dim(proj_left, start_a, CL, 1)
            part_b = lax.dynamic_slice_in_dim(proj_right, start_b, CL, 1)
            same = (first == second).astype(jnp.float32)
            force_a, energy_a, force_b = tile_terms(left, right, part_a, part_b, same, jnp.float32(1.0), w_radial, w_hidden, w_out)
            added = jnp.concatenate([force_a, energy_a[None, :]], 0)
            firsts = lax.dynamic_update_slice_in_dim(firsts, lax.dynamic_slice_in_dim(firsts, start_a, CL, 1) + added, start_a, 1)
            seconds = lax.dynamic_update_slice_in_dim(seconds, lax.dynamic_slice_in_dim(seconds, start_b, CL, 1) + force_b, start_b, 1)
            return (firsts, seconds)
        return (lax.cond(is_live, work, lambda carry: carry, (firsts, seconds)), None)
    start = (jnp.zeros((4, NB), jnp.float32), jnp.zeros((3, NB), jnp.float32))
    (firsts, seconds), unused = lax.scan(step, start, jnp.arange(NTILES, dtype=jnp.int32))
    return (firsts[:3] + seconds, firsts[3])
```

```python
import functools
import math

import jax
import jax.numpy as jnp
from jax import lax
from jax.experimental import pallas as pl
from jax.experimental.pallas import tpu as pltpu
from jax.sharding import PartitionSpec as P

CL = 128
SOFT = 0.01
RANGE = 6.0
GROUP = 8
MESH = pl.DeviceIdType.MESH
F32 = jnp.float32
BF16 = jnp.bfloat16


def peers(nrow, ncol, i, j):
    along_col = [(d, lax.rem(j + d, ncol)) for d in range(1, ncol)]
    along_row = [(d, lax.rem(i + d, nrow)) for d in range(1, nrow)]
    return along_col, along_row


def enter(i, j, along_col, along_row):
    barrier = pltpu.get_barrier_semaphore()
    for _, c in along_col:
        pl.semaphore_signal(barrier, inc=1, device_id=(i, c), device_id_type=MESH)
    for _, r in along_row:
        pl.semaphore_signal(barrier, inc=1, device_id=(r, j), device_id_type=MESH)
    return barrier, len(along_col) + len(along_row)


def gather_kernel(
    nrow, ncol, pos_ref, feat_ref, fill_ref, wl_ref, wr_ref,
    rowc_ref, rowp_ref, colc_ref, colp_ref, send_sem, recv_sem,
):
    i = lax.axis_index("row")
    j = lax.axis_index("col")
    along_col, along_row = peers(nrow, ncol, i, j)
    barrier, count = enter(i, j, along_col, along_row)
    beads = pos_ref.shape[1]
    lane = lax.broadcasted_iota(jnp.int32, (1, CL), 1)
    live = jnp.concatenate(
        [(lane < fill_ref[k]).astype(F32) for k in range(beads // CL)], 1
    )
    coords = jnp.concatenate([pos_ref[...], live, jnp.zeros((4, beads), F32)], 0)
    rowc_ref[j] = coords
    colc_ref[i] = coords
    dims = (((0,), (0,)), ((), ()))
    feats = feat_ref[...]
    rowp_ref[j] = lax.dot_general(wl_ref[...], feats, dims, preferred_element_type=F32).astype(BF16)
    colp_ref[i] = lax.dot_general(wr_ref[...], feats, dims, preferred_element_type=F32).astype(BF16)
    pl.semaphore_wait(barrier, count)
    copies = []
    for d, r in along_row:
        for ref in (colp_ref, colc_ref):
            copies.append((ref.at[i], (r, j)))
    for d, c in along_col:
        for ref in (rowp_ref, rowc_ref):
            copies.append((ref.at[j], (i, c)))
    started = []
    for k, (ref, target) in enumerate(copies):
        copy = pltpu.make_async_remote_copy(
            src_ref=ref, dst_ref=ref, send_sem=send_sem.at[k], recv_sem=recv_sem.at[k],
            device_id=target, device_id_type=MESH,
        )
        copy.start()
        started.append(copy)
    for copy in started:
        copy.wait()


def scatter_kernel(
    nrow, ncol, first_ref, second_ref, force_ref, energy_ref, row_in, col_in, send_sem, recv_sem
):
    i = lax.axis_index("row")
    j = lax.axis_index("col")
    along_col, along_row = peers(nrow, ncol, i, j)
    barrier, count = enter(i, j, along_col, along_row)
    pl.semaphore_wait(barrier, count)
    started = []
    for d, r in along_row:
        started.append((second_ref.at[r], col_in.at[d], (r, j)))
    for d, c in along_col:
        started.append((first_ref.at[c], row_in.at[d], (i, c)))
    copies = []
    for k, (src, dst, target) in enumerate(started):
        copy = pltpu.make_async_remote_copy(
            src_ref=src, dst_ref=dst, send_sem=send_sem.at[k], recv_sem=recv_sem.at[k],
            device_id=target, device_id_type=MESH,
        )
        copy.start()
        copies.append(copy)
    total = first_ref[j]
    other = second_ref[i]
    for copy in copies:
        copy.wait()
    for d in range(1, ncol):
        total = total + row_in[d]
    for d in range(1, nrow):
        other = other + col_in[d]
    force_ref[...] = total[:3] + other[:3]
    energy_ref[...] = total[3:4]


def tile_kernel(
    cpd, ncol, tiles_ref, count_ref, rowc_ref, rowp_ref, colc_ref, colp_ref,
    wrad_ref, whid_ref, wout_ref, first_ref, second_ref,
    acc_ref, left_ref, proj_ref, base_ref,
):
    row = lax.axis_index("row")
    col = lax.axis_index("col")
    hidden, nbasis = wrad_ref.shape
    clusters = acc_ref.shape[0]
    spacing = RANGE / (nbasis - 1)
    scale = math.sqrt(math.log2(math.e))
    back = -2.0 / (spacing * scale)
    live_count = count_ref[0]
    acc_ref[...] = jnp.zeros_like(acc_ref)
    second_ref[...] = jnp.zeros_like(second_ref)

    wide = jnp.concatenate(
        [0.5 * wrad_ref[...], jnp.zeros((hidden, CL - nbasis), F32)], 1
    )
    base_ref[...] = wide
    whid = whid_ref[...] * jnp.asarray(0.5, BF16)
    wout = wout_ref[...].astype(F32)
    spread = jnp.concatenate([wout] * GROUP, 1)
    spread = jnp.broadcast_to(spread, (GROUP, GROUP * hidden))
    owner = lax.broadcasted_iota(jnp.int32, (GROUP, GROUP * hidden), 1) // hidden
    which = lax.broadcasted_iota(jnp.int32, (GROUP, GROUP * hidden), 0)
    wout_wide = jnp.where(owner == which, spread, 0.0).astype(BF16)
    centers = lax.broadcasted_iota(jnp.int32, (nbasis, CL), 0).astype(F32) * scale
    lanes64 = lax.broadcasted_iota(jnp.int32, (hidden, CL), 1)
    lanes = lax.broadcasted_iota(jnp.int32, (GROUP, CL), 1)
    subl = lax.broadcasted_iota(jnp.int32, (GROUP, CL), 0)
    pick = lax.broadcasted_iota(jnp.int32, (16, 2 * CL), 0)
    side = lax.broadcasted_iota(jnp.int32, (16, 2 * CL), 1) < CL

    @pl.loop(0, live_count)
    def _(slot):
        first = tiles_ref[slot, 0]
        other = tiles_ref[slot, 1]
        col_a = first // cpd
        row_b = other // cpd
        at_a = pl.ds(pl.multiple_of(first % cpd * CL, CL), CL)
        at_b = pl.ds(pl.multiple_of(other % cpd * CL, CL), CL)
        same = jnp.logical_and(
            jnp.logical_and(col_a == col, row_b == row), first % cpd == other % cpd
        ).astype(F32)
        left = rowc_ref[col_a, :, at_a]
        left_ref[:, :8] = left.T
        proj_ref[...] = 0.5 * rowp_ref[col_a, :, at_a].astype(F32)
        right = colc_ref[row_b, :, at_b]
        pair_b = 0.5 * colp_ref[row_b, :, at_b].astype(F32)
        beads = jnp.sum(left[3:4]).astype(jnp.int32)
        chunks = (beads + GROUP - 1) // GROUP

        def chunk(c, carry):
            start = pl.multiple_of(c * GROUP, GROUP)
            mine = left_ref[pl.ds(start, GROUP), :]
            dx = mine[:, 0:1] - right[0:1]
            dy = mine[:, 1:2] - right[1:2]
            dz = mine[:, 2:3] - right[2:3]
            dist = jnp.sqrt(dx * dx + dy * dy + dz * dz + SOFT)
            mask = mine[:, 3:4] * right[3:4] * (
                1.0 - same * (subl + c * GROUP == lanes).astype(F32)
            )
            scaled = dist * (scale / spacing)
            rolled = pltpu.roll(proj_ref[...], lax.rem(nbasis - c * GROUP + CL, CL), 1)
            lhs = jnp.where(lanes64 < nbasis, base_ref[...], rolled)[:, : nbasis + 16].astype(BF16)
            lasts = []
            for a in range(GROUP):
                off = scaled[a : a + 1] - centers
                basis = jnp.exp2(-(off * off))
                lift = basis * off
                x1 = jnp.concatenate(
                    [
                        jnp.concatenate([basis, lift], 1).astype(BF16),
                        jnp.where(jnp.logical_and(pick == a, side), 1.0, 0.0).astype(BF16),
                    ],
                    0,
                )
                y1 = jnp.dot(lhs, x1, preferred_element_type=F32)
                h = y1[:, :CL] + pair_b
                t = jnp.tanh(h)
                u = 1.0 + t
                s = h * u
                d = u + s - t * s
                x2 = jnp.concatenate([s, d * y1[:, CL:]], 1).astype(BF16)
                y2 = jnp.dot(whid, x2, preferred_element_type=F32)
                h = y2[:, :CL]
                t = jnp.tanh(h)
                u = 1.0 + t
                s = h * u
                d = u + s - t * s
                lasts.append(jnp.concatenate([s, d * y2[:, CL:]], 1).astype(BF16))
            y3 = jnp.dot(wout_wide, jnp.concatenate(lasts, 0), preferred_element_type=F32)
            weight = (back * mask) * y3[:, CL:] / dist
            wx = weight * dx
            wy = weight * dy
            wz = weight * dz
            energy = jnp.sum(mask * y3[:, :CL], 1, keepdims=True)
            fx = -jnp.sum(wx, 1, keepdims=True)
            fy = -jnp.sum(wy, 1, keepdims=True)
            fz = -jnp.sum(wz, 1, keepdims=True)
            added = jnp.where(
                lanes == 0, fx, jnp.where(lanes == 1, fy, jnp.where(lanes == 2, fz, energy))
            )
            rows = pl.ds(start, GROUP)
            acc_ref[first, rows, :] = acc_ref[first, rows, :] + added
            return (carry[0] + wx, carry[1] + wy, carry[2] + wz)

        zero = jnp.zeros((GROUP, CL), F32)
        sums = lax.fori_loop(0, chunks, chunk, (zero, zero, zero))
        for k in range(3):
            total = jnp.sum(sums[k], 0, keepdims=True)
            second_ref[row_b, k : k + 1, at_b] = second_ref[row_b, k : k + 1, at_b] + total

    for k in range(clusters):
        place = (k // cpd, slice(None), slice(k % cpd * CL, k % cpd * CL + CL))
        first_ref[place] = acc_ref[k][:, :8].T


def body(nrow, ncol, positions, features, fill, tiles, tile_count, w_radial, w_left, w_right, w_hidden, w_out):
    beads = positions.shape[1]
    hidden = w_radial.shape[0]
    cpd = fill.shape[0]
    vmem = pl.BlockSpec(memory_space=pltpu.VMEM)
    smem = pl.BlockSpec(memory_space=pltpu.SMEM)
    sends = nrow + ncol - 2
    gathered = pl.pallas_call(
        functools.partial(gather_kernel, nrow, ncol),
        name="gather",
        out_shape=(
            jax.ShapeDtypeStruct((ncol, 8, beads), F32),
            jax.ShapeDtypeStruct((ncol, hidden, beads), BF16),
            jax.ShapeDtypeStruct((nrow, 8, beads), F32),
            jax.ShapeDtypeStruct((nrow, hidden, beads), BF16),
        ),
        in_specs=[vmem, vmem, smem, vmem, vmem],
        out_specs=(vmem,) * 4,
        scratch_shapes=[
            pltpu.SemaphoreType.DMA((2 * sends,)),
            pltpu.SemaphoreType.DMA((2 * sends,)),
        ],
        compiler_params=pltpu.CompilerParams(collective_id=0, has_side_effects=True),
    )(positions, features, fill, w_left, w_right)
    firsts, seconds = pl.pallas_call(
        functools.partial(tile_kernel, cpd, ncol),
        name="tiles",
        out_shape=(
            jax.ShapeDtypeStruct((ncol, 8, beads), F32),
            jax.ShapeDtypeStruct((nrow, 8, beads), F32),
        ),
        in_specs=[smem, smem] + [vmem] * 7,
        out_specs=(vmem, vmem),
        scratch_shapes=[
            pltpu.VMEM((ncol * cpd, CL, CL), F32),
            pltpu.VMEM((CL, CL), F32),
            pltpu.VMEM((hidden, CL), F32),
            pltpu.VMEM((hidden, CL), F32),
        ],
    )(tiles, tile_count, *gathered, w_radial, w_hidden, w_out[None, :])
    forces, energy = pl.pallas_call(
        functools.partial(scatter_kernel, nrow, ncol),
        name="scatter",
        out_shape=(
            jax.ShapeDtypeStruct((3, beads), F32),
            jax.ShapeDtypeStruct((1, beads), F32),
        ),
        in_specs=[vmem, vmem],
        out_specs=(vmem, vmem),
        scratch_shapes=[
            pltpu.VMEM((ncol, 8, beads), F32),
            pltpu.VMEM((nrow, 8, beads), F32),
            pltpu.SemaphoreType.DMA((sends,)),
            pltpu.SemaphoreType.DMA((sends,)),
        ],
        compiler_params=pltpu.CompilerParams(collective_id=1, has_side_effects=True),
    )(firsts, seconds)
    return forces, energy[0]


def solution(mesh):
    nrow, ncol = mesh.shape["row"], mesh.shape["col"]
    return jax.shard_map(
        functools.partial(body, nrow, ncol),
        mesh=mesh,
        in_specs=(
            P(None, ("row", "col")),
            P(None, ("row", "col")),
            P(("row", "col")),
            P(("row", "col"), None),
            P(("row", "col")),
            P(),
            P(),
            P(),
            P(),
            P(),
        ),
        out_specs=(P(None, ("row", "col")), P(("row", "col"))),
        check_vma=False,
    )
```

```python
import functools
import math

import jax
import jax.numpy as jnp
from jax import lax
from jax.experimental import pallas as pl
from jax.experimental.pallas import tpu as pltpu
from jax.sharding import PartitionSpec as P

CL = 128
SOFT = 0.01
RANGE = 6.0
GROUP = 8
STEP = 16
PICK = 16
MESH = pl.DeviceIdType.MESH
F32 = jnp.float32
BF16 = jnp.bfloat16


def peers(nrow, ncol, i, j):
    along_col = [(d, lax.rem(j + d, ncol)) for d in range(1, ncol)]
    along_row = [(d, lax.rem(i + d, nrow)) for d in range(1, nrow)]
    return along_col, along_row


def enter(i, j, along_col, along_row):
    barrier = pltpu.get_barrier_semaphore()
    for _, c in along_col:
        pl.semaphore_signal(barrier, inc=1, device_id=(i, c), device_id_type=MESH)
    for _, r in along_row:
        pl.semaphore_signal(barrier, inc=1, device_id=(r, j), device_id_type=MESH)
    return barrier, len(along_col) + len(along_row)


def gather_kernel(
    nrow, ncol, pos_ref, feat_ref, fill_ref, wl_ref, wr_ref,
    rowc_ref, rowp_ref, colc_ref, colp_ref, send_sem, recv_sem,
):
    i = lax.axis_index("row")
    j = lax.axis_index("col")
    along_col, along_row = peers(nrow, ncol, i, j)
    barrier, count = enter(i, j, along_col, along_row)
    beads = pos_ref.shape[1]
    lane = lax.broadcasted_iota(jnp.int32, (1, CL), 1)
    live = jnp.concatenate(
        [(lane < fill_ref[k]).astype(F32) for k in range(beads // CL)], 1
    )
    coords = jnp.concatenate([pos_ref[...], live, jnp.zeros((4, beads), F32)], 0)
    rowc_ref[j] = coords
    colc_ref[i] = coords
    dims = (((1,), (0,)), ((), ()))
    feats = feat_ref[...]
    rowp_ref[j] = lax.dot_general(wl_ref[...], feats, dims, preferred_element_type=F32).astype(BF16)
    colp_ref[i] = lax.dot_general(wr_ref[...], feats, dims, preferred_element_type=F32).astype(BF16)
    pl.semaphore_wait(barrier, count)
    copies = []
    for d, r in along_row:
        for ref in (colp_ref, colc_ref):
            copies.append((ref.at[i], (r, j)))
    for d, c in along_col:
        for ref in (rowp_ref, rowc_ref):
            copies.append((ref.at[j], (i, c)))
    started = []
    for k, (ref, target) in enumerate(copies):
        copy = pltpu.make_async_remote_copy(
            src_ref=ref, dst_ref=ref, send_sem=send_sem.at[k], recv_sem=recv_sem.at[k],
            device_id=target, device_id_type=MESH,
        )
        copy.start()
        started.append(copy)
    for copy in started:
        copy.wait()


def scatter_kernel(
    nrow, ncol, first_ref, second_ref, force_ref, energy_ref, row_in, col_in, send_sem, recv_sem
):
    i = lax.axis_index("row")
    j = lax.axis_index("col")
    along_col, along_row = peers(nrow, ncol, i, j)
    barrier, count = enter(i, j, along_col, along_row)
    pl.semaphore_wait(barrier, count)
    started = []
    for d, r in along_row:
        started.append((second_ref.at[r], col_in.at[d], (r, j)))
    for d, c in along_col:
        started.append((first_ref.at[c], row_in.at[d], (i, c)))
    copies = []
    for k, (src, dst, target) in enumerate(started):
        copy = pltpu.make_async_remote_copy(
            src_ref=src, dst_ref=dst, send_sem=send_sem.at[k], recv_sem=recv_sem.at[k],
            device_id=target, device_id_type=MESH,
        )
        copy.start()
        copies.append(copy)
    total = first_ref[j]
    other = second_ref[i]
    for copy in copies:
        copy.wait()
    for d in range(1, ncol):
        total = total + row_in[d]
    for d in range(1, nrow):
        other = other + col_in[d]
    force_ref[...] = total[:3] + other[:3]
    energy_ref[...] = total[3:4]


def tile_kernel(
    cpd, ncol, tiles_ref, count_ref, rowc_ref, rowp_ref, colc_ref, colp_ref,
    wrad_ref, whid_ref, wout_ref, first_ref, second_ref,
    acc_ref, dist_ref, last_ref, proj_ref, pair_ref, base_ref, pick_ref,
):
    row = lax.axis_index("row")
    col = lax.axis_index("col")
    nbasis, hidden = wrad_ref.shape
    clusters = acc_ref.shape[0]
    spacing = RANGE / (nbasis - 1)
    scale = math.sqrt(math.log2(math.e))
    back = -2.0 / (spacing * scale)
    live_count = count_ref[0]
    acc_ref[...] = jnp.zeros_like(acc_ref)
    second_ref[...] = jnp.zeros_like(second_ref)

    wide = jnp.concatenate(
        [0.5 * wrad_ref[...].T, jnp.zeros((hidden, CL - nbasis), F32)], 1
    )
    base_ref[...] = wide
    whid = whid_ref[...] * jnp.asarray(0.5, BF16)
    wout = wout_ref[...].astype(F32)
    spread = jnp.concatenate([wout] * GROUP, 1)
    spread = jnp.broadcast_to(spread, (GROUP, GROUP * hidden))
    owner = lax.broadcasted_iota(jnp.int32, (GROUP, GROUP * hidden), 1) // hidden
    which = lax.broadcasted_iota(jnp.int32, (GROUP, GROUP * hidden), 0)
    wout_wide = jnp.where(owner == which, spread, 0.0).astype(BF16)
    centers = lax.broadcasted_iota(jnp.int32, (nbasis, CL), 0).astype(F32) * scale
    lanes64 = lax.broadcasted_iota(jnp.int32, (hidden, CL), 1)
    lanes = lax.broadcasted_iota(jnp.int32, (CL, CL), 1)
    ident = (lax.broadcasted_iota(jnp.int32, (CL, CL), 0) == lanes).astype(F32)
    pick = lax.broadcasted_iota(jnp.int32, (PICK, 2 * CL), 0)
    side = lax.broadcasted_iota(jnp.int32, (PICK, 2 * CL), 1) < CL
    for a in range(STEP):
        pick_ref[a] = jnp.where(jnp.logical_and(pick == a, side), 1.0, 0.0).astype(BF16)

    @pl.loop(0, live_count)
    def _(slot):
        first = tiles_ref[0, slot]
        other = tiles_ref[1, slot]
        col_a = first // cpd
        row_b = other // cpd
        at_a = pl.ds(pl.multiple_of(first % cpd * CL, CL), CL)
        at_b = pl.ds(pl.multiple_of(other % cpd * CL, CL), CL)
        same = jnp.logical_and(
            jnp.logical_and(col_a == col, row_b == row), first % cpd == other % cpd
        ).astype(F32)
        left = rowc_ref[col_a, :, at_a]
        mine = left.T
        proj_ref[...] = 0.5 * rowp_ref[col_a, :, at_a].astype(F32)
        right = colc_ref[row_b, :, at_b]
        pair_ref[...] = 0.5 * colp_ref[row_b, :, at_b].astype(F32)
        beads = jnp.sum(left[3:4]).astype(jnp.int32)
        chunks = (beads + STEP - 1) // STEP
        dx = mine[:, 0:1] - right[0:1]
        dy = mine[:, 1:2] - right[1:2]
        dz = mine[:, 2:3] - right[2:3]
        dist = jnp.sqrt(dx * dx + dy * dy + dz * dz + SOFT)
        dist_ref[...] = dist * (scale / spacing)

        @pl.loop(0, chunks)
        def _(c):
            start = pl.multiple_of(c * STEP, STEP)
            rolled = pltpu.roll(proj_ref[...], lax.rem(nbasis - c * STEP + CL, CL), 1)
            lhs = jnp.where(lanes64 < nbasis, base_ref[...], rolled)[:, : nbasis + PICK].astype(BF16)
            for half in range(0, STEP, GROUP):
                rows = pl.ds(pl.multiple_of(start + half, GROUP), GROUP)
                scaled = dist_ref[rows, :]
                lasts = []
                for a in range(GROUP):
                    off = scaled[a : a + 1] - centers
                    basis = jnp.exp2(-(off * off))
                    lift = basis * off
                    x1 = jnp.concatenate(
                        [jnp.concatenate([basis, lift], 1).astype(BF16), pick_ref[half + a]], 0
                    )
                    y1 = jnp.dot(lhs, x1, preferred_element_type=F32)
                    h = y1[:, :CL] + pair_ref[...]
                    t = jnp.tanh(h)
                    u = 1.0 + t
                    s = h * u
                    d = u + s - t * s
                    x2 = jnp.concatenate([s, d * y1[:, CL:]], 1).astype(BF16)
                    y2 = jnp.dot(whid, x2, preferred_element_type=F32)
                    h = y2[:, :CL]
                    t = jnp.tanh(h)
                    u = 1.0 + t
                    s = h * u
                    d = u + s - t * s
                    lasts.append(jnp.concatenate([s, d * y2[:, CL:]], 1).astype(BF16))
                last_ref[rows, :] = jnp.dot(
                    wout_wide, jnp.concatenate(lasts, 0), preferred_element_type=F32
                )

        dist = dist_ref[...] * (spacing / scale)
        both = jnp.logical_and(mine[:, 3:4] * right[3:4] > 0.5, same * ident < 0.5)
        weight = jnp.where(both, back * last_ref[:, CL:] / dist, 0.0)
        phi = jnp.where(both, last_ref[:, :CL], 0.0)
        wx = weight * dx
        wy = weight * dy
        wz = weight * dz
        energy = jnp.sum(phi, 1, keepdims=True)
        fx = -jnp.sum(wx, 1, keepdims=True)
        fy = -jnp.sum(wy, 1, keepdims=True)
        fz = -jnp.sum(wz, 1, keepdims=True)
        acc_ref[first] = acc_ref[first] + jnp.where(
            lanes == 0, fx, jnp.where(lanes == 1, fy, jnp.where(lanes == 2, fz, energy))
        )
        for k, part in enumerate((wx, wy, wz)):
            total = jnp.sum(part, 0, keepdims=True)
            second_ref[row_b, k : k + 1, at_b] = second_ref[row_b, k : k + 1, at_b] + total

    for k in range(clusters):
        place = (k // cpd, slice(None), slice(k % cpd * CL, k % cpd * CL + CL))
        first_ref[place] = acc_ref[k][:, :8].T


def body(nrow, ncol, positions, features, fill, tiles, tile_count, w_radial, w_left, w_right, w_hidden, w_out):
    beads = positions.shape[1]
    hidden = w_radial.shape[0]
    cpd = fill.shape[0]
    vmem = pl.BlockSpec(memory_space=pltpu.VMEM)
    smem = pl.BlockSpec(memory_space=pltpu.SMEM)
    sends = nrow + ncol - 2
    gathered = pl.pallas_call(
        functools.partial(gather_kernel, nrow, ncol),
        name="gather",
        out_shape=(
            jax.ShapeDtypeStruct((ncol, 8, beads), F32),
            jax.ShapeDtypeStruct((ncol, hidden, beads), BF16),
            jax.ShapeDtypeStruct((nrow, 8, beads), F32),
            jax.ShapeDtypeStruct((nrow, hidden, beads), BF16),
        ),
        in_specs=[vmem, vmem, smem, vmem, vmem],
        out_specs=(vmem,) * 4,
        scratch_shapes=[
            pltpu.SemaphoreType.DMA((2 * sends,)),
            pltpu.SemaphoreType.DMA((2 * sends,)),
        ],
        compiler_params=pltpu.CompilerParams(collective_id=0, has_side_effects=True),
    )(positions, features, fill, w_left.T, w_right.T)
    firsts, seconds = pl.pallas_call(
        functools.partial(tile_kernel, cpd, ncol),
        name="tiles",
        out_shape=(
            jax.ShapeDtypeStruct((ncol, 8, beads), F32),
            jax.ShapeDtypeStruct((nrow, 8, beads), F32),
        ),
        in_specs=[smem, smem] + [vmem] * 7,
        out_specs=(vmem, vmem),
        scratch_shapes=[
            pltpu.VMEM((ncol * cpd, CL, CL), F32),
            pltpu.VMEM((CL, CL), F32),
            pltpu.VMEM((CL, 2 * CL), F32),
            pltpu.VMEM((hidden, CL), F32),
            pltpu.VMEM((hidden, CL), F32),
            pltpu.VMEM((hidden, CL), F32),
            pltpu.VMEM((STEP, PICK, 2 * CL), BF16),
        ],
    )(tiles.T, tile_count, *gathered, w_radial.T, w_hidden, w_out[None, :])
    forces, energy = pl.pallas_call(
        functools.partial(scatter_kernel, nrow, ncol),
        name="scatter",
        out_shape=(
            jax.ShapeDtypeStruct((3, beads), F32),
            jax.ShapeDtypeStruct((1, beads), F32),
        ),
        in_specs=[vmem, vmem],
        out_specs=(vmem, vmem),
        scratch_shapes=[
            pltpu.VMEM((ncol, 8, beads), F32),
            pltpu.VMEM((nrow, 8, beads), F32),
            pltpu.SemaphoreType.DMA((sends,)),
            pltpu.SemaphoreType.DMA((sends,)),
        ],
        compiler_params=pltpu.CompilerParams(collective_id=1, has_side_effects=True),
    )(firsts, seconds)
    return forces, energy[0]


def solution(mesh):
    nrow, ncol = mesh.shape["row"], mesh.shape["col"]
    return jax.shard_map(
        functools.partial(body, nrow, ncol),
        mesh=mesh,
        in_specs=(
            P(None, ("row", "col")),
            P(None, ("row", "col")),
            P(("row", "col")),
            P(("row", "col"), None),
            P(("row", "col")),
            P(),
            P(),
            P(),
            P(),
            P(),
        ),
        out_specs=(P(None, ("row", "col")), P(("row", "col"))),
        check_vma=False,
    )
```

```python
import functools
import math

import jax
import jax.numpy as jnp
from jax import lax
from jax.experimental import pallas as pl
from jax.experimental.pallas import tpu as pltpu
from jax.sharding import PartitionSpec as P

CL = 128
SOFT = 0.01
RANGE = 6.0
GROUP = 8
STEP = 16
PICK = 16
MESH = pl.DeviceIdType.MESH
F32 = jnp.float32
BF16 = jnp.bfloat16


def peers(nrow, ncol, i, j):
    along_col = [(d, lax.rem(j + d, ncol)) for d in range(1, ncol)]
    along_row = [(d, lax.rem(i + d, nrow)) for d in range(1, nrow)]
    return along_col, along_row


def enter(i, j, along_col, along_row):
    barrier = pltpu.get_barrier_semaphore()
    for _, c in along_col:
        pl.semaphore_signal(barrier, inc=1, device_id=(i, c), device_id_type=MESH)
    for _, r in along_row:
        pl.semaphore_signal(barrier, inc=1, device_id=(r, j), device_id_type=MESH)
    return barrier, len(along_col) + len(along_row)


def gather_kernel(
    nrow, ncol, pos_ref, feat_ref, fill_ref, wl_ref, wr_ref,
    rowc_ref, rowp_ref, colc_ref, colp_ref, send_sem, recv_sem,
):
    i = lax.axis_index("row")
    j = lax.axis_index("col")
    along_col, along_row = peers(nrow, ncol, i, j)
    barrier, count = enter(i, j, along_col, along_row)
    beads = pos_ref.shape[1]
    lane = lax.broadcasted_iota(jnp.int32, (1, CL), 1)
    live = jnp.concatenate(
        [(lane < fill_ref[k]).astype(F32) for k in range(beads // CL)], 1
    )
    coords = jnp.concatenate([pos_ref[...], live, jnp.zeros((4, beads), F32)], 0)
    rowc_ref[j] = coords
    colc_ref[i] = coords
    dims = (((1,), (0,)), ((), ()))
    feats = feat_ref[...]
    rowp_ref[j] = lax.dot_general(wl_ref[...], feats, dims, preferred_element_type=F32).astype(BF16)
    colp_ref[i] = lax.dot_general(wr_ref[...], feats, dims, preferred_element_type=F32).astype(BF16)
    pl.semaphore_wait(barrier, count)
    copies = []
    for d, r in along_row:
        for ref in (colp_ref, colc_ref):
            copies.append((ref.at[i], (r, j)))
    for d, c in along_col:
        for ref in (rowp_ref, rowc_ref):
            copies.append((ref.at[j], (i, c)))
    started = []
    for k, (ref, target) in enumerate(copies):
        copy = pltpu.make_async_remote_copy(
            src_ref=ref, dst_ref=ref, send_sem=send_sem.at[k], recv_sem=recv_sem.at[k],
            device_id=target, device_id_type=MESH,
        )
        copy.start()
        started.append(copy)
    for copy in started:
        copy.wait()


def scatter_kernel(
    nrow, ncol, first_ref, second_ref, force_ref, energy_ref, row_in, col_in, send_sem, recv_sem
):
    i = lax.axis_index("row")
    j = lax.axis_index("col")
    along_col, along_row = peers(nrow, ncol, i, j)
    barrier, count = enter(i, j, along_col, along_row)
    pl.semaphore_wait(barrier, count)
    started = []
    for d, r in along_row:
        started.append((second_ref.at[r], col_in.at[d], (r, j)))
    for d, c in along_col:
        started.append((first_ref.at[c], row_in.at[d], (i, c)))
    copies = []
    for k, (src, dst, target) in enumerate(started):
        copy = pltpu.make_async_remote_copy(
            src_ref=src, dst_ref=dst, send_sem=send_sem.at[k], recv_sem=recv_sem.at[k],
            device_id=target, device_id_type=MESH,
        )
        copy.start()
        copies.append(copy)
    total = first_ref[j]
    other = second_ref[i]
    for copy in copies:
        copy.wait()
    for d in range(1, ncol):
        total = total + row_in[d]
    for d in range(1, nrow):
        other = other + col_in[d]
    force_ref[...] = total[:3] + other[:3]
    energy_ref[...] = total[3:4]


def tile_kernel(
    cpd, ncol, tiles_ref, count_ref, rowc_ref, rowp_ref, colc_ref, colp_ref,
    wrad_ref, whid_ref, wout_ref, first_ref, second_ref,
    acc_ref, dist_ref, phi_ref, slope_ref, proj_ref, pair_ref, base_ref, wout_ref8, pick_ref,
):
    row = lax.axis_index("row")
    col = lax.axis_index("col")
    nbasis, hidden = wrad_ref.shape
    clusters = acc_ref.shape[0]
    spacing = RANGE / (nbasis - 1)
    scale = math.sqrt(math.log2(math.e))
    back = -2.0 / (spacing * scale)
    live_count = count_ref[0]
    acc_ref[...] = jnp.zeros_like(acc_ref)
    second_ref[...] = jnp.zeros_like(second_ref)

    wide = jnp.concatenate(
        [0.5 * wrad_ref[...].T, jnp.zeros((hidden, CL - nbasis), F32)], 1
    )
    base_ref[...] = wide
    whid = whid_ref[...] * jnp.asarray(0.5, BF16)
    wout = jnp.broadcast_to(wout_ref[...].astype(F32), (8, hidden)).T
    wout_ref8[...] = jnp.broadcast_to(wout[:, 0:1], (hidden, CL))
    centers = lax.broadcasted_iota(jnp.int32, (nbasis, CL), 0).astype(F32) * scale
    lanes64 = lax.broadcasted_iota(jnp.int32, (hidden, CL), 1)
    lanes = lax.broadcasted_iota(jnp.int32, (CL, CL), 1)
    ident = (lax.broadcasted_iota(jnp.int32, (CL, CL), 0) == lanes).astype(F32)
    pick = lax.broadcasted_iota(jnp.int32, (PICK, 2 * CL), 0)
    side = lax.broadcasted_iota(jnp.int32, (PICK, 2 * CL), 1) < CL
    for a in range(STEP):
        pick_ref[a] = jnp.where(jnp.logical_and(pick == a, side), 1.0, 0.0).astype(BF16)

    @pl.loop(0, live_count)
    def _(slot):
        first = tiles_ref[0, slot]
        other = tiles_ref[1, slot]
        col_a = first // cpd
        row_b = other // cpd
        at_a = pl.ds(pl.multiple_of(first % cpd * CL, CL), CL)
        at_b = pl.ds(pl.multiple_of(other % cpd * CL, CL), CL)
        same = jnp.logical_and(
            jnp.logical_and(col_a == col, row_b == row), first % cpd == other % cpd
        ).astype(F32)
        left = rowc_ref[col_a, :, at_a]
        mine = left.T
        proj_ref[...] = 0.5 * rowp_ref[col_a, :, at_a].astype(F32)
        right = colc_ref[row_b, :, at_b]
        pair_ref[...] = 0.5 * colp_ref[row_b, :, at_b].astype(F32)
        beads = jnp.sum(left[3:4]).astype(jnp.int32)
        chunks = (beads + STEP - 1) // STEP
        dx = mine[:, 0:1] - right[0:1]
        dy = mine[:, 1:2] - right[1:2]
        dz = mine[:, 2:3] - right[2:3]
        dist = jnp.sqrt(dx * dx + dy * dy + dz * dz + SOFT)
        dist_ref[...] = dist * (scale / spacing)

        @pl.loop(0, chunks)
        def _(c):
            start = pl.multiple_of(c * STEP, STEP)
            rolled = pltpu.roll(proj_ref[...], lax.rem(nbasis - c * STEP + CL, CL), 1)
            lhs = jnp.where(lanes64 < nbasis, base_ref[...], rolled)[:, : nbasis + PICK].astype(BF16)
            for half in range(0, STEP, GROUP):
                rows = pl.ds(pl.multiple_of(start + half, GROUP), GROUP)
                scaled = dist_ref[rows, :]
                for a in range(GROUP):
                    off = scaled[a : a + 1] - centers
                    basis = jnp.exp2(-(off * off))
                    lift = basis * off
                    x1 = jnp.concatenate(
                        [jnp.concatenate([basis, lift], 1).astype(BF16), pick_ref[half + a]], 0
                    )
                    y1 = jnp.dot(lhs, x1, preferred_element_type=F32)
                    h = y1[:, :CL] + pair_ref[...]
                    t = jnp.tanh(h)
                    u = 1.0 + t
                    s = h * u
                    d = u + s - t * s
                    x2 = jnp.concatenate([s, d * y1[:, CL:]], 1).astype(BF16)
                    y2 = jnp.dot(whid, x2, preferred_element_type=F32)
                    h = y2[:, :CL]
                    t = jnp.tanh(h)
                    u = (1.0 + t) * wout_ref8[...]
                    s = h * u
                    g = (u + (1.0 - t) * s) * y2[:, CL:]
                    spot = pl.ds(pl.multiple_of(start * 8, 8) + (half + a) * 8, 8)
                    phi_ref[spot, :] = jnp.sum(s.reshape(hidden // 8, 8, CL), 0)
                    slope_ref[spot, :] = jnp.sum(g.reshape(hidden // 8, 8, CL), 0)

        dist = dist_ref[...] * (spacing / scale)
        slope = slope_ref[pl.ds(0, CL, stride=8), :]
        phi = phi_ref[pl.ds(0, CL, stride=8), :]
        for k in range(1, 8):
            slope = slope + slope_ref[pl.ds(k, CL, stride=8), :]
            phi = phi + phi_ref[pl.ds(k, CL, stride=8), :]
        both = jnp.logical_and(mine[:, 3:4] * right[3:4] > 0.5, same * ident < 0.5)
        weight = jnp.where(both, back * slope / dist, 0.0)
        phi = jnp.where(both, phi, 0.0)
        wx = weight * dx
        wy = weight * dy
        wz = weight * dz
        energy = jnp.sum(phi, 1, keepdims=True)
        fx = -jnp.sum(wx, 1, keepdims=True)
        fy = -jnp.sum(wy, 1, keepdims=True)
        fz = -jnp.sum(wz, 1, keepdims=True)
        acc_ref[first] = acc_ref[first] + jnp.where(
            lanes == 0, fx, jnp.where(lanes == 1, fy, jnp.where(lanes == 2, fz, energy))
        )
        for k, part in enumerate((wx, wy, wz)):
            total = jnp.sum(part, 0, keepdims=True)
            second_ref[row_b, k : k + 1, at_b] = second_ref[row_b, k : k + 1, at_b] + total

    for k in range(clusters):
        place = (k // cpd, slice(None), slice(k % cpd * CL, k % cpd * CL + CL))
        first_ref[place] = acc_ref[k][:, :8].T


def body(nrow, ncol, positions, features, fill, tiles, tile_count, w_radial, w_left, w_right, w_hidden, w_out):
    beads = positions.shape[1]
    hidden = w_radial.shape[0]
    cpd = fill.shape[0]
    vmem = pl.BlockSpec(memory_space=pltpu.VMEM)
    smem = pl.BlockSpec(memory_space=pltpu.SMEM)
    sends = nrow + ncol - 2
    gathered = pl.pallas_call(
        functools.partial(gather_kernel, nrow, ncol),
        name="gather",
        out_shape=(
            jax.ShapeDtypeStruct((ncol, 8, beads), F32),
            jax.ShapeDtypeStruct((ncol, hidden, beads), BF16),
            jax.ShapeDtypeStruct((nrow, 8, beads), F32),
            jax.ShapeDtypeStruct((nrow, hidden, beads), BF16),
        ),
        in_specs=[vmem, vmem, smem, vmem, vmem],
        out_specs=(vmem,) * 4,
        scratch_shapes=[
            pltpu.SemaphoreType.DMA((2 * sends,)),
            pltpu.SemaphoreType.DMA((2 * sends,)),
        ],
        compiler_params=pltpu.CompilerParams(collective_id=0, has_side_effects=True),
    )(positions, features, fill, w_left.T, w_right.T)
    firsts, seconds = pl.pallas_call(
        functools.partial(tile_kernel, cpd, ncol),
        name="tiles",
        out_shape=(
            jax.ShapeDtypeStruct((ncol, 8, beads), F32),
            jax.ShapeDtypeStruct((nrow, 8, beads), F32),
        ),
        in_specs=[smem, smem] + [vmem] * 7,
        out_specs=(vmem, vmem),
        scratch_shapes=[
            pltpu.VMEM((ncol * cpd, CL, CL), F32),
            pltpu.VMEM((CL, CL), F32),
            pltpu.VMEM((CL * 8, CL), F32),
            pltpu.VMEM((CL * 8, CL), F32),
            pltpu.VMEM((hidden, CL), F32),
            pltpu.VMEM((hidden, CL), F32),
            pltpu.VMEM((hidden, CL), F32),
            pltpu.VMEM((hidden, CL), F32),
            pltpu.VMEM((STEP, PICK, 2 * CL), BF16),
        ],
    )(tiles.T, tile_count, *gathered, w_radial.T, w_hidden, w_out[None, :])
    forces, energy = pl.pallas_call(
        functools.partial(scatter_kernel, nrow, ncol),
        name="scatter",
        out_shape=(
            jax.ShapeDtypeStruct((3, beads), F32),
            jax.ShapeDtypeStruct((1, beads), F32),
        ),
        in_specs=[vmem, vmem],
        out_specs=(vmem, vmem),
        scratch_shapes=[
            pltpu.VMEM((ncol, 8, beads), F32),
            pltpu.VMEM((nrow, 8, beads), F32),
            pltpu.SemaphoreType.DMA((sends,)),
            pltpu.SemaphoreType.DMA((sends,)),
        ],
        compiler_params=pltpu.CompilerParams(collective_id=1, has_side_effects=True),
    )(firsts, seconds)
    return forces, energy[0]


def solution(mesh):
    nrow, ncol = mesh.shape["row"], mesh.shape["col"]
    return jax.shard_map(
        functools.partial(body, nrow, ncol),
        mesh=mesh,
        in_specs=(
            P(None, ("row", "col")),
            P(None, ("row", "col")),
            P(("row", "col")),
            P(("row", "col"), None),
            P(("row", "col")),
            P(),
            P(),
            P(),
            P(),
            P(),
        ),
        out_specs=(P(None, ("row", "col")), P(("row", "col"))),
        check_vma=False,
    )
```

```python
import functools
import math

import jax
import jax.numpy as jnp
from jax import lax
from jax.experimental import pallas as pl
from jax.experimental.pallas import tpu as pltpu
from jax.sharding import PartitionSpec as P

CL = 128
SOFT = 0.01
RANGE = 6.0
GROUP = 8
STEP = 16
PICK = 16
MESH = pl.DeviceIdType.MESH
F32 = jnp.float32
BF16 = jnp.bfloat16


def peers(nrow, ncol, i, j):
    along_col = [(d, lax.rem(j + d, ncol)) for d in range(1, ncol)]
    along_row = [(d, lax.rem(i + d, nrow)) for d in range(1, nrow)]
    return along_col, along_row


def enter(i, j, along_col, along_row):
    barrier = pltpu.get_barrier_semaphore()
    for _, c in along_col:
        pl.semaphore_signal(barrier, inc=1, device_id=(i, c), device_id_type=MESH)
    for _, r in along_row:
        pl.semaphore_signal(barrier, inc=1, device_id=(r, j), device_id_type=MESH)
    return barrier, len(along_col) + len(along_row)


def gather_kernel(
    nrow, ncol, inner, pos_ref, feat_ref, fill_ref, wl_ref, wr_ref,
    rowc_ref, rowp_ref, colc_ref, colp_ref, send_sem, recv_sem,
):
    i = lax.axis_index("row")
    j = lax.axis_index("col")
    outer = nrow // inner
    at_out = i // inner
    at_in = i % inner
    cols = [lax.rem(j + d, ncol) for d in range(1, ncol)]
    outs = [lax.rem(at_out + d, outer) * inner + at_in for d in range(1, outer)]
    origins = [lax.rem(at_out + outer - d, outer) * inner + at_in for d in range(1, outer)]
    mates = [at_out * inner + lax.rem(at_in + d, inner) for d in range(1, inner)]
    barrier = pltpu.get_barrier_semaphore()
    for target in [(r, j) for r in outs + mates] + [(i, c) for c in cols]:
        pl.semaphore_signal(barrier, inc=1, device_id=target, device_id_type=MESH)
    beads = pos_ref.shape[1]
    lane = lax.broadcasted_iota(jnp.int32, (1, CL), 1)
    live = jnp.concatenate(
        [(lane < fill_ref[k]).astype(F32) for k in range(beads // CL)], 1
    )
    coords = jnp.concatenate([pos_ref[...], live], 0)
    rowc_ref[j] = coords
    colc_ref[i] = coords
    dims = (((1,), (0,)), ((), ()))
    feats = feat_ref[...]
    rowp_ref[j] = lax.dot_general(wl_ref[...], feats, dims, preferred_element_type=F32).astype(BF16)
    colp_ref[i] = lax.dot_general(wr_ref[...], feats, dims, preferred_element_type=F32).astype(BF16)
    pl.semaphore_wait(barrier, len(outs) + len(mates) + len(cols))
    started = []

    def send(refs, slot, target):
        copies = []
        for ref in refs:
            k = len(started)
            copy = pltpu.make_async_remote_copy(
                src_ref=ref.at[slot], dst_ref=ref.at[slot],
                send_sem=send_sem.at[k], recv_sem=recv_sem.at[k],
                device_id=target, device_id_type=MESH,
            )
            copy.start()
            started.append(copy)
            copies.append(copy)
        return copies

    late = []
    hops = [send((colp_ref, colc_ref), i, (r, j)) for r in outs]
    for r in mates:
        late += send((colp_ref, colc_ref), i, (r, j))
    for c in cols:
        late += send((rowp_ref, rowc_ref), j, (i, c))
    for copies, origin in zip(hops, origins):
        for copy in copies:
            copy.wait_recv()
        for r in mates:
            late += send((colp_ref, colc_ref), origin, (r, j))
    for copies in hops:
        for copy in copies:
            copy.wait_send()
    for copy in late:
        copy.wait()


def scatter_kernel(
    nrow, ncol, first_ref, second_ref, force_ref, energy_ref, row_in, col_in, send_sem, recv_sem
):
    i = lax.axis_index("row")
    j = lax.axis_index("col")
    along_col, along_row = peers(nrow, ncol, i, j)
    barrier, count = enter(i, j, along_col, along_row)
    pl.semaphore_wait(barrier, count)
    started = []
    for d, r in along_row:
        started.append((second_ref.at[r], col_in.at[d], (r, j)))
    for d, c in along_col:
        started.append((first_ref.at[c], row_in.at[d], (i, c)))
    copies = []
    for k, (src, dst, target) in enumerate(started):
        copy = pltpu.make_async_remote_copy(
            src_ref=src, dst_ref=dst, send_sem=send_sem.at[k], recv_sem=recv_sem.at[k],
            device_id=target, device_id_type=MESH,
        )
        copy.start()
        copies.append(copy)
    total = first_ref[j]
    other = second_ref[i]
    for copy in copies:
        copy.wait()
    for d in range(1, ncol):
        total = total + row_in[d]
    for d in range(1, nrow):
        other = other + col_in[d]
    force_ref[...] = total[:3] + other[:3]
    energy_ref[...] = total[3:4]


def tile_kernel(
    cpd, ncol, tiles_ref, count_ref, rowc_ref, rowp_ref, colc_ref, colp_ref,
    wrad_ref, whid_ref, wout_ref, first_ref, second_ref,
    acc_ref, dist_ref, phi_ref, slope_ref, proj_ref, pair_ref, base_ref, wout_ref8, pick_ref,
):
    row = lax.axis_index("row")
    col = lax.axis_index("col")
    nbasis, hidden = wrad_ref.shape
    clusters = acc_ref.shape[0]
    spacing = RANGE / (nbasis - 1)
    scale = math.sqrt(math.log2(math.e))
    back = -2.0 / (spacing * scale)
    live_count = count_ref[0]
    acc_ref[...] = jnp.zeros_like(acc_ref)
    second_ref[...] = jnp.zeros_like(second_ref)

    wide = jnp.concatenate(
        [0.5 * wrad_ref[...].T, jnp.zeros((hidden, CL - nbasis), F32)], 1
    )
    base_ref[...] = wide
    whid = whid_ref[...] * jnp.asarray(0.5, BF16)
    wout = jnp.broadcast_to(wout_ref[...].astype(F32), (8, hidden)).T
    wout_ref8[...] = jnp.broadcast_to(wout[:, 0:1], (hidden, CL))
    centers = lax.broadcasted_iota(jnp.int32, (nbasis, CL), 0).astype(F32) * scale
    lanes64 = lax.broadcasted_iota(jnp.int32, (hidden, CL), 1)
    lanes = lax.broadcasted_iota(jnp.int32, (CL, CL), 1)
    ident = (lax.broadcasted_iota(jnp.int32, (CL, CL), 0) == lanes).astype(F32)
    pick = lax.broadcasted_iota(jnp.int32, (PICK, 2 * CL), 0)
    side = lax.broadcasted_iota(jnp.int32, (PICK, 2 * CL), 1) < CL
    for a in range(STEP):
        pick_ref[a] = jnp.where(jnp.logical_and(pick == a, side), 1.0, 0.0).astype(BF16)

    one = jnp.asarray(1.0, BF16)

    @pl.loop(0, live_count)
    def _(slot):
        first = tiles_ref[0, slot]
        other = tiles_ref[1, slot]
        col_a = first // cpd
        row_b = other // cpd
        at_a = pl.ds(pl.multiple_of(first % cpd * CL, CL), CL)
        at_b = pl.ds(pl.multiple_of(other % cpd * CL, CL), CL)
        same = jnp.logical_and(
            jnp.logical_and(col_a == col, row_b == row), first % cpd == other % cpd
        ).astype(F32)
        left = rowc_ref[col_a, :, at_a]
        mine = jnp.concatenate([left, left], 0).T
        proj_ref[...] = 0.5 * rowp_ref[col_a, :, at_a].astype(F32)
        right = colc_ref[row_b, :, at_b]
        pair_ref[...] = 0.5 * colp_ref[row_b, :, at_b].astype(F32)
        beads = jnp.sum(left[3:4]).astype(jnp.int32)
        chunks = (beads + STEP - 1) // STEP
        dx = mine[:, 0:1] - right[0:1]
        dy = mine[:, 1:2] - right[1:2]
        dz = mine[:, 2:3] - right[2:3]
        dist = jnp.sqrt(dx * dx + dy * dy + dz * dz + SOFT)
        dist_ref[...] = dist * (scale / spacing)

        def step(start):
            rolled = pltpu.roll(proj_ref[...], lax.rem(nbasis - start + CL, CL), 1)
            lhs = jnp.where(lanes64 < nbasis, base_ref[...], rolled)[:, : nbasis + PICK].astype(BF16)
            for half in range(0, STEP, GROUP):
                rows = pl.ds(pl.multiple_of(start + half, GROUP), GROUP)
                scaled = dist_ref[rows, :]
                for a in range(GROUP):
                    off = scaled[a : a + 1] - centers
                    basis = jnp.exp2(-(off * off))
                    lift = basis * off
                    x1 = jnp.concatenate(
                        [jnp.concatenate([basis, lift], 1).astype(BF16), pick_ref[half + a]], 0
                    )
                    y1 = jnp.dot(lhs, x1, preferred_element_type=F32)
                    h = (y1[:, :CL] + pair_ref[...]).astype(BF16)
                    e = y1[:, CL:].astype(BF16)
                    t = jnp.tanh(h)
                    u = one + t
                    s = h * u
                    d = u + (one - t) * s
                    x2 = jnp.concatenate([s, d * e], 1)
                    y2 = jnp.dot(whid, x2, preferred_element_type=F32)
                    h = y2[:, :CL]
                    t = jnp.tanh(h)
                    u = (1.0 + t) * wout_ref8[...]
                    s = h * u
                    g = (u + (1.0 - t) * s) * y2[:, CL:]
                    spot = pl.ds(pl.multiple_of(start * 8, 8) + (half + a) * 8, 8)
                    phi_ref[spot, :] = jnp.sum(s.reshape(hidden // 8, 8, CL), 0)
                    slope_ref[spot, :] = jnp.sum(g.reshape(hidden // 8, 8, CL), 0)

        @pl.loop(0, chunks // 2)
        def _(c):
            start = pl.multiple_of(c * (2 * STEP), 2 * STEP)
            step(start)
            step(start + STEP)

        @pl.when(chunks % 2 == 1)
        def _():
            step(pl.multiple_of((chunks - 1) * STEP, STEP))

        dist = dist_ref[...] * (spacing / scale)
        slope = slope_ref[pl.ds(0, CL, stride=8), :]
        phi = phi_ref[pl.ds(0, CL, stride=8), :]
        for k in range(1, 8):
            slope = slope + slope_ref[pl.ds(k, CL, stride=8), :]
            phi = phi + phi_ref[pl.ds(k, CL, stride=8), :]
        both = jnp.logical_and(mine[:, 3:4] * right[3:4] > 0.5, same * ident < 0.5)
        weight = jnp.where(both, back * slope / dist, 0.0)
        phi = jnp.where(both, phi, 0.0)
        wx = weight * dx
        wy = weight * dy
        wz = weight * dz
        energy = jnp.sum(phi, 1, keepdims=True)
        fx = -jnp.sum(wx, 1, keepdims=True)
        fy = -jnp.sum(wy, 1, keepdims=True)
        fz = -jnp.sum(wz, 1, keepdims=True)
        acc_ref[first] = acc_ref[first] + jnp.where(
            lanes == 0, fx, jnp.where(lanes == 1, fy, jnp.where(lanes == 2, fz, energy))
        )
        for k, part in enumerate((wx, wy, wz)):
            total = jnp.sum(part, 0, keepdims=True)
            second_ref[row_b, k : k + 1, at_b] = second_ref[row_b, k : k + 1, at_b] + total

    for k in range(clusters):
        place = (k // cpd, slice(None), slice(k % cpd * CL, k % cpd * CL + CL))
        first_ref[place] = acc_ref[k][:, :8].T


def body(nrow, ncol, positions, features, fill, tiles, tile_count, w_radial, w_left, w_right, w_hidden, w_out):
    beads = positions.shape[1]
    hidden = w_radial.shape[0]
    cpd = fill.shape[0]
    vmem = pl.BlockSpec(memory_space=pltpu.VMEM)
    smem = pl.BlockSpec(memory_space=pltpu.SMEM)
    sends = nrow + ncol - 2
    inner = 2 if nrow % 2 == 0 else 1
    gathered = pl.pallas_call(
        functools.partial(gather_kernel, nrow, ncol, inner),
        name="gather",
        out_shape=(
            jax.ShapeDtypeStruct((ncol, 4, beads), F32),
            jax.ShapeDtypeStruct((ncol, hidden, beads), BF16),
            jax.ShapeDtypeStruct((nrow, 4, beads), F32),
            jax.ShapeDtypeStruct((nrow, hidden, beads), BF16),
        ),
        in_specs=[vmem, vmem, smem, vmem, vmem],
        out_specs=(vmem,) * 4,
        scratch_shapes=[
            pltpu.SemaphoreType.DMA((2 * sends,)),
            pltpu.SemaphoreType.DMA((2 * sends,)),
        ],
        compiler_params=pltpu.CompilerParams(collective_id=0, has_side_effects=True),
    )(positions, features, fill, w_left.T, w_right.T)
    firsts, seconds = pl.pallas_call(
        functools.partial(tile_kernel, cpd, ncol),
        name="tiles",
        out_shape=(
            jax.ShapeDtypeStruct((ncol, 8, beads), F32),
            jax.ShapeDtypeStruct((nrow, 8, beads), F32),
        ),
        in_specs=[smem, smem] + [vmem] * 7,
        out_specs=(vmem, vmem),
        scratch_shapes=[
            pltpu.VMEM((ncol * cpd, CL, CL), F32),
            pltpu.VMEM((CL, CL), F32),
            pltpu.VMEM((CL * 8, CL), F32),
            pltpu.VMEM((CL * 8, CL), F32),
            pltpu.VMEM((hidden, CL), F32),
            pltpu.VMEM((hidden, CL), F32),
            pltpu.VMEM((hidden, CL), F32),
            pltpu.VMEM((hidden, CL), F32),
            pltpu.VMEM((STEP, PICK, 2 * CL), BF16),
        ],
    )(tiles.T, tile_count, *gathered, w_radial.T, w_hidden, w_out[None, :])
    forces, energy = pl.pallas_call(
        functools.partial(scatter_kernel, nrow, ncol),
        name="scatter",
        out_shape=(
            jax.ShapeDtypeStruct((3, beads), F32),
            jax.ShapeDtypeStruct((1, beads), F32),
        ),
        in_specs=[vmem, vmem],
        out_specs=(vmem, vmem),
        scratch_shapes=[
            pltpu.VMEM((ncol, 8, beads), F32),
            pltpu.VMEM((nrow, 8, beads), F32),
            pltpu.SemaphoreType.DMA((sends,)),
            pltpu.SemaphoreType.DMA((sends,)),
        ],
        compiler_params=pltpu.CompilerParams(collective_id=1, has_side_effects=True),
    )(firsts, seconds)
    return forces, energy[0]


def solution(mesh):
    nrow, ncol = mesh.shape["row"], mesh.shape["col"]
    return jax.shard_map(
        functools.partial(body, nrow, ncol),
        mesh=mesh,
        in_specs=(
            P(None, ("row", "col")),
            P(None, ("row", "col")),
            P(("row", "col")),
            P(("row", "col"), None),
            P(("row", "col")),
            P(),
            P(),
            P(),
            P(),
            P(),
        ),
        out_specs=(P(None, ("row", "col")), P(("row", "col"))),
        check_vma=False,
    )
```
